256 devices in a mesh: teacher: 4 (over x), dp: 2 (over core), vocab: 32 (over z, y).
Axes of the slice: x: 4, y: 4, z: 8, core: 2. Of those that a mesh axis runs over, the one named last changes fastest.
Arguments:
- teacher_of_seq: int32 [16], replicated, may hold values from 0 to 3, as said below
- teacher_hidden: bfloat16 [4, 512, 4096], P('teacher', 'vocab', 'dp'), may hold values from -160 to 160, as said below
- teacher_weight: bfloat16 [4, 4096, 65536], P('teacher', 'dp', 'vocab'), may hold values from -0.09375 to 0.09375
- student_hidden: bfloat16 [1024, 3072], P(None, ('teacher', 'dp')), may hold values from -160 to 160
- student_weight: bfloat16 [3072, 65536], P(('teacher', 'dp'), 'vocab'), may hold values from -0.109375 to 0.109375
Outputs:
- kl_rows: float32 [1024], P(('teacher', 'dp'))
- grad_weight: bfloat16 [3072, 65536], P(('teacher', 'dp'), 'vocab')
- grad_hidden: bfloat16 [1024, 3072], P('vocab', ('teacher', 'dp'))
The draws below stay inside these ranges and needn't reach their ends.
Inputs may be any that keep to these rules, and one draw needn't show every extreme that they name: `teacher_of_seq`: every teacher has at least one sequence and one teacher has exactly 8. `teacher_hidden`: slots from 64 times the teacher's number of sequences on are not read.
All inputs are finite; a program needn't handle non-finite values.
Results may differ from the reference program's by a relative error of at most 0.01225.
The reference program's roundings to bfloat16 on the way (of `teacher_logits` and `grad_logits`) count: a program that leaves them out, or rounds other values in their place, can miss the bound.
Values may be sent and summed in bfloat16 or wider, within the bound.
No kernel may reach another device: no remote copies, remote signals or barrier semaphores. Data moves between devices by JAX's collectives and lax.ppermute only.
A program may use at most 128 MiB of HBM per device.

```python
import jax
import jax.numpy as jnp
from jax import lax

SEQS = 16
POS = 64
TD = 4096
SD = 3072
TEACHERS = 4
CAP = 512
ROWS = 1024
VOCAB = 65536


def draw_teacher_of_seq(key, part):
    half = SEQS // 2
    hottest = jax.random.randint(jax.random.fold_in(key, 11), (), 0, TEACHERS)
    cuts = jnp.sort(jax.random.permutation(jax.random.fold_in(key, 12), half - 1)[:2] + 1)
    others = jnp.stack([cuts[0], cuts[1] - cuts[0], half - cuts[1]]).astype(jnp.int32)
    teacher_ids = jnp.arange(TEACHERS, dtype=jnp.int32)
    ranked = jnp.clip(teacher_ids - (teacher_ids > hottest).astype(jnp.int32), 0, 2)
    counts = jnp.where(teacher_ids == hottest, half, others[ranked]).astype(jnp.int32)
    ends = jnp.cumsum(counts)
    sequence = jnp.arange(SEQS, dtype=jnp.int32)
    labels = jnp.sum((sequence[:, None] >= ends[None, :]).astype(jnp.int32), axis=1).astype(jnp.int32)
    pick = jax.random.randint(jax.random.fold_in(key, 13), (), 0, 2).astype(jnp.int32)
    target = ((pick + 2) % TEACHERS).astype(jnp.int32)
    first = (pick * (SEQS // 4)).astype(jnp.int32)
    scores = jax.random.permutation(jax.random.fold_in(key, 14), SEQS).astype(jnp.int32)
    is_target = labels == target
    smaller = scores[None, :] < scores[:, None]
    rank_other = jnp.sum((smaller & jnp.logical_not(is_target)[None, :]).astype(jnp.int32), axis=1)
    rank_target = jnp.sum((smaller & is_target[None, :]).astype(jnp.int32), axis=1)
    leading = is_target & (rank_target == 0)
    placed = jnp.logical_not(is_target) & (rank_other < first)
    sort_keys = jnp.where(placed, rank_other, jnp.where(leading, first, SEQS + scores)).astype(jnp.int32)
    order = jnp.argsort(sort_keys, stable=True)
    return labels[order].astype(jnp.int32)


def scaled_rows(key, shape):
    values = jnp.clip(jax.random.normal(jax.random.fold_in(key, 21), shape, jnp.float32), -4.0, 4.0)
    return values


def draw_teacher_hidden(key, part):
    return scaled_rows(key, (TEACHERS, CAP, TD)).astype(jnp.bfloat16)


def draw_student_hidden(key, part):
    return scaled_rows(jax.random.fold_in(key, 31), (ROWS, SD)).astype(jnp.bfloat16)


def levels(stream_key, dims, shards, least, high):
    factor_of = 1.0
    for axis_at, parts in shards:
        heights = jax.random.uniform(jax.random.fold_in(jax.random.fold_in(stream_key, 6), axis_at), (parts,), jnp.float32, least / len(shards), high / len(shards))
        factor_of = factor_of * jnp.repeat(jnp.exp(heights), dims[axis_at] // parts).reshape((-1,) + (1,) * (len(dims) - 1 - axis_at))
    return factor_of


def gaussian(rng, dims, deviation, limit, shards=(), kind=jnp.bfloat16):
    level = levels(rng, dims, shards, -0.22, 0.18) if shards else 1.0
    array = jax.random.normal(rng, dims, jnp.float32) * deviation * level
    return jnp.minimum(jnp.maximum(array, -limit), limit).astype(kind)


def setup_inputs(seed: int = 0) -> dict:
    keys = jax.random.split(jax.random.key(seed), 6)
    return {
        "teacher_of_seq": draw_teacher_of_seq(jax.random.fold_in(keys[5], 71), 0),
        "teacher_hidden": draw_teacher_hidden(jax.random.fold_in(keys[5], 71), 0),
        "teacher_weight": gaussian(keys[2], (TEACHERS, TD, VOCAB), TD ** -0.5, 0.09375, ((0, 4), (1, 2), (2, 32))),
        "student_hidden": draw_student_hidden(jax.random.fold_in(keys[5], 71), 0),
        "student_weight": gaussian(keys[4], (SD, VOCAB), SD ** -0.5, 0.109375, ((0, 8), (1, 32))),
    }


def head_rows(pair):
    hidden, weight = pair
    return jnp.dot(hidden, weight, preferred_element_type=jnp.float32).astype(jnp.bfloat16)


def row_lse(logits):
    row_max = jnp.max(logits, axis=1)
    total = jnp.sum(jnp.exp(logits - row_max[:, None]), axis=1)
    return row_max + jnp.log(total)


def reference(teacher_of_seq, teacher_hidden, teacher_weight, student_hidden, student_weight):
    sequence_ids = jnp.arange(SEQS, dtype=jnp.int32)
    same_before = (teacher_of_seq[None, :] == teacher_of_seq[:, None]) & (sequence_ids[None, :] < sequence_ids[:, None])
    earlier = jnp.sum(same_before.astype(jnp.int32), axis=1).astype(jnp.int32)
    row_teacher = jnp.repeat(teacher_of_seq, POS).astype(jnp.int32)
    within = (jnp.arange(ROWS, dtype=jnp.int32) % POS).astype(jnp.int32)
    slot_index = (jnp.repeat(earlier, POS) * POS + within).astype(jnp.int32)
    slot_logits = lax.map(head_rows, (teacher_hidden, teacher_weight))
    teacher_logits = slot_logits[row_teacher, slot_index].astype(jnp.float32)
    student_logits = jnp.dot(student_hidden, student_weight, preferred_element_type=jnp.float32)
    teacher_lse = row_lse(teacher_logits)
    student_lse = row_lse(student_logits)
    teacher_prob = jnp.exp(teacher_logits - teacher_lse[:, None])
    cross_term = jnp.sum(teacher_prob * (teacher_logits - student_logits), axis=1)
    kl_rows = cross_term - teacher_lse + student_lse
    grad_logits = (VOCAB * (jnp.exp(student_logits - student_lse[:, None]) - teacher_prob)).astype(jnp.bfloat16)
    grad_weight = jnp.dot(student_hidden.T, grad_logits, preferred_element_type=jnp.float32).astype(jnp.bfloat16)
    grad_hidden = jnp.dot(grad_logits, student_weight.T, preferred_element_type=jnp.float32).astype(jnp.bfloat16)
    return (kl_rows, grad_weight, grad_hidden)
```

```python
import jax
import jax.numpy as jnp
from jax import lax
from jax.sharding import Mesh
from jax.sharding import PartitionSpec as P


X, D, Z, Y = "teacher", "dp", "vocab_0", "vocab_1"
F32, BF16 = jnp.float32, jnp.bfloat16


def moved(x, axis, shift):
    n = lax.axis_size(axis)
    return lax.ppermute(x, axis, [(i, (i + shift) % n) for i in range(n)])


def dot(a, b):
    return jnp.dot(a, b, preferred_element_type=F32)


def gathered_hidden(h):
    nz = lax.axis_size(Z)
    own = jnp.concatenate([h] + [moved(h, Y, k) for k in range(1, lax.axis_size(Y))], axis=0)
    right, left = [own], [own]
    for _ in range(nz // 2 - 1):
        right.append(moved(right[-1], Z, 1))
        left.append(moved(left[-1], Z, -1))
    half = own.shape[0] // 2
    far = jnp.concatenate([moved(right[-1][:half], Z, 1), moved(left[-1][half:], Z, -1)], axis=0)
    return right, far, left


def merged(parts):
    tm = parts[0][0]
    sm = parts[0][3]
    for p in parts[1:]:
        tm = jnp.maximum(tm, p[0])
        sm = jnp.maximum(sm, p[3])
    ts = tc = ss = 0.0
    for p in parts:
        scale = jnp.exp(p[0] - tm)
        ts += p[1] * scale
        tc += p[2] * scale
        ss += p[4] * jnp.exp(p[3] - sm)
    return jnp.stack([tm, ts, tc, sm, ss])


def shards(teacher_of_seq, teacher_hidden, teacher_weight, student_hidden, student_weight):
    nx, nd, nz, ny = (lax.axis_size(a) for a in (X, D, Z, Y))
    x, d, z, y = (lax.axis_index(a) for a in (X, D, Z, Y))
    rows = student_hidden.shape[0]
    cols = student_weight.shape[1]
    features = student_weight.shape[0]
    block = cols // (nx * nd)
    vocab_total = cols * nz * ny
    seqs = teacher_of_seq.shape[0]

    def columns(w, k):
        at = lax.rem(x + k, nx) * block
        mine = lax.dynamic_slice_in_dim(w, d * (cols // nd) + at, block, 1)
        other = lax.dynamic_slice_in_dim(w, (1 - d) * (cols // nd) + at, block, 1)
        return mine, other

    right, far, left = gathered_hidden(teacher_hidden[0])

    sw = [columns(student_weight, k) for k in range(nx)]
    mine = dot(student_hidden, sw[0][0])
    other = dot(student_hidden, sw[0][1])
    for k in range(1, nx):
        w = moved(jnp.concatenate(sw[k], axis=1), X, k)
        h = moved(student_hidden, X, k)
        mine += dot(h, w[:, :block])
        other += dot(h, w[:, block:])
    student = mine + moved(other, D, 1)

    tw = [columns(teacher_weight[0], k) for k in range(nx)]
    w_mine = jnp.concatenate([t[0] for t in tw], axis=1)
    w_other = jnp.concatenate([t[1] for t in tw], axis=1)
    hidden = jnp.concatenate(right + [far] + left[:0:-1], axis=0)
    t_other = moved(dot(hidden, w_other), D, 1)
    t_mine = dot(hidden, w_mine)
    got = []
    for k in range(nx):
        at = slice(k * block, (k + 1) * block)
        part = (t_mine[:, at] + t_other[:, at]).astype(BF16)
        got.append(moved(part, X, k) if k else part)
    slots = jnp.concatenate(got, axis=0)

    sequence = jnp.arange(seqs, dtype=jnp.int32)
    same_before = (teacher_of_seq[None, :] == teacher_of_seq[:, None]) & (
        sequence[None, :] < sequence[:, None]
    )
    earlier = jnp.sum(same_before.astype(jnp.int32), axis=1)
    piece = teacher_hidden.shape[1]
    from_x = lax.rem(x - teacher_of_seq + nx, nx)
    from_z = lax.rem(z - earlier + nz, nz)
    from_y = lax.rem(y - jnp.arange(ny, dtype=jnp.int32) + ny, ny)
    source = ((from_x * nz + from_z) * ny)[:, None] + from_y[None, :]
    teacher = jnp.take(slots.reshape(-1, piece, block), source.reshape(-1), axis=0)
    teacher = teacher.reshape(rows, block).astype(F32)

    tm = jnp.max(teacher, axis=1)
    sm = jnp.max(student, axis=1)
    te = jnp.exp(teacher - tm[:, None])
    stats = jnp.stack(
        [
            tm,
            jnp.sum(te, axis=1),
            jnp.sum(te * (teacher - student), axis=1),
            sm,
            jnp.sum(jnp.exp(student - sm[:, None]), axis=1),
        ]
    )
    for axis in (D, X, Y, Z):
        parts = [stats] + [moved(stats, axis, k) for k in range(1, lax.axis_size(axis))]
        stats = merged(parts)
    teacher_lse = stats[0] + jnp.log(stats[1])
    student_lse = stats[3] + jnp.log(stats[4])
    kl = stats[2] / stats[1] - teacher_lse + student_lse
    kl_block = rows // (nx * nd)
    kl_rows = lax.dynamic_slice_in_dim(kl, (x * nd + d) * kl_block, kl_block)

    gradient = (
        vocab_total
        * (jnp.exp(student - student_lse[:, None]) - jnp.exp(teacher - teacher_lse[:, None]))
    ).astype(BF16)

    near = [gradient] + [moved(gradient, X, k) for k in range(1, nx)]
    across = [moved(g, D, 1) for g in near]
    order = [(-k) % nx for k in range(nx)]
    everything = jnp.concatenate(near + across, axis=1)
    w_all = jnp.concatenate([sw[k][0] for k in order] + [sw[k][1] for k in order], axis=1)
    partial = lax.dot_general(
        everything, w_all, (((1,), (1,)), ((), ())), preferred_element_type=F32
    ).astype(BF16)

    piece_rows = rows // (nz * ny)
    by_y = partial.reshape(nz, ny, piece_rows, features)
    total = 0.0
    for k in range(ny):
        part = lax.dynamic_index_in_dim(by_y, lax.rem(y + k, ny), 1, keepdims=False)
        total += (moved(part, Y, k) if k else part).astype(F32)
    by_z = total.astype(BF16)
    total = 0.0
    for k in range(nz):
        part = lax.dynamic_index_in_dim(by_z, lax.rem(z + k, nz), 0, keepdims=False)
        total += (moved(part, Z, k) if k else part).astype(F32)
    grad_hidden = total.astype(BF16)

    grad_weight = lax.dot_general(
        student_hidden, everything, (((0,), (0,)), ((), ())), preferred_element_type=F32
    ).astype(BF16)
    place = lax.rem(x - jnp.arange(nx, dtype=jnp.int32) + nx, nx)
    blocks = [
        lax.dynamic_slice_in_dim(
            grad_weight, ((h + d) % nd * nx + place[c]) * block, block, 1
        )
        for h in range(nd)
        for c in range(nx)
    ]
    grad_weight = jnp.concatenate(blocks, axis=1)
    return (kl_rows, grad_weight, grad_hidden)


def solution(mesh):
    split = Mesh(
        mesh.devices.reshape(mesh.shape["teacher"], mesh.shape["dp"], 8, 4), (X, D, Z, Y)
    )
    return jax.shard_map(
        shards,
        mesh=split,
        in_specs=(
            P(),
            P(X, (Z, Y), D),
            P(X, D, (Z, Y)),
            P(None, (X, D)),
            P((X, D), (Z, Y)),
        ),
        out_specs=(P((X, D)), P((X, D), (Z, Y)), P((Z, Y), (X, D))),
        check_vma=False,
    )
```

```python
import functools


import jax
import jax.numpy as jnp
from jax import lax
from jax.experimental import pallas as pl
from jax.experimental.pallas import tpu as pltpu
from jax.sharding import Mesh
from jax.sharding import PartitionSpec as P


X, D, Z, Y = "teacher", "dp", "vocab_0", "vocab_1"
F32, BF16 = jnp.float32, jnp.bfloat16


def moved(x, axis, shift):
    n = lax.axis_size(axis)
    return lax.ppermute(x, axis, [(i, (i + shift) % n) for i in range(n)])


def dot(a, b):
    return jnp.dot(a, b, preferred_element_type=F32)


def copies(x, axis):
    return jnp.broadcast_to(x[None], (lax.axis_size(axis), *x.shape))


def to_all(x, axis):
    return lax.all_to_all(copies(x, axis), axis, 0, 0, tiled=True)


def lse(values):
    top = jnp.max(values, axis=0)
    return top + jnp.log(jnp.sum(jnp.exp(values - top), axis=0))


def merged(parts):
    teacher = lse(parts[:, 0])
    cross = jnp.sum(parts[:, 1] * jnp.exp(parts[:, 0] - teacher), axis=0)
    return jnp.stack([teacher, cross, lse(parts[:, 2])])


VMEM = pl.BlockSpec(memory_space=pltpu.VMEM)


def cost(m, k, n, out_bytes):
    return pl.CostEstimate(
        flops=2 * m * k * n, bytes_accessed=2 * (m * k + k * n) + out_bytes * m * n, transcendentals=0
    )


def product_kernel(count, tile, at, *refs):
    left, right = refs[:count], refs[count : -2]
    out, joined = refs[-2:]
    depth = left[0].shape[1]
    for k in range(count):
        if at is None:
            joined[pl.ds(k * depth, depth), :] = right[k][...]
        else:
            rows = pl.ds(pl.multiple_of(at[k], depth), depth)
            joined[pl.ds(k * depth, depth), :] = right[0][rows, :]

    @pl.loop(0, out.shape[0] // tile)
    def _(i):
        rows = pl.ds(pl.multiple_of(i * tile, tile), tile)
        wide = jnp.concatenate([part[rows, :] for part in left], axis=1)
        out[rows, :] = dot(wide, joined[...]).astype(out.dtype)


def product(left, right, dtype, at=None, tile=256):
    count = len(left)
    rows, depth = left[0].shape
    cols = right[0].shape[1]
    kernel = functools.partial(product_kernel, count, tile)
    if at is None:
        kernel = functools.partial(product_kernel, count, tile, None)
    return pl.pallas_call(
        kernel,
        out_shape=jax.ShapeDtypeStruct((rows, cols), dtype),
        grid_spec=pltpu.PrefetchScalarGridSpec(
            num_scalar_prefetch=0 if at is None else 1,
            grid=(),
            in_specs=[VMEM] * (count + len(right)),
            out_specs=VMEM,
            scratch_shapes=[pltpu.VMEM((count * depth, cols), BF16)],
        ),
        cost_estimate=cost(rows, count * depth, cols, jnp.dtype(dtype).itemsize),
        compiler_params=pltpu.CompilerParams(vmem_limit_bytes=20 << 20),
    )(*(() if at is None else (at,)), *left, *right)


def weight_kernel(count, at, h, *refs):
    gradients, out = refs[:count], refs[count]
    for k in range(count):

        @pl.when(pl.program_id(0) == k)
        def _():
            out[...] = dot(h[...], gradients[k][...]).astype(out.dtype)


def weight_gradient(at, h, gradients):
    rows, block = gradients[0].shape
    features, count = h.shape[0], len(gradients)
    return pl.pallas_call(
        functools.partial(weight_kernel, count),
        out_shape=jax.ShapeDtypeStruct((features, block * count), BF16),
        grid_spec=pltpu.PrefetchScalarGridSpec(
            num_scalar_prefetch=1,
            grid=(count,),
            in_specs=[VMEM] * (1 + count),
            out_specs=pl.BlockSpec((features, block), lambda k, at: (0, at[k] // block)),
        ),
        cost_estimate=cost(features, rows, block * count, 2),
        compiler_params=pltpu.CompilerParams(vmem_limit_bytes=16 << 20),
        name="weight_gradient",
    )(at, h, *gradients)


def shards(teacher_of_seq, teacher_hidden, teacher_weight, student_hidden, student_weight):
    nx, nd, nz, ny = (lax.axis_size(a) for a in (X, D, Z, Y))
    x, d, _, y = (lax.axis_index(a) for a in (X, D, Z, Y))
    rows = student_hidden.shape[0]
    cols = student_weight.shape[1]
    features = student_weight.shape[0]
    block = cols // (nx * nd)
    half = cols // nd
    vocab_total = cols * nz * ny
    seqs = teacher_of_seq.shape[0]
    piece = teacher_hidden.shape[1]

    def columns(w, k):
        at = lax.rem(x + k, nx) * block
        mine = lax.dynamic_slice_in_dim(w, d * half + at, block, 1)
        other = lax.dynamic_slice_in_dim(w, (1 - d) * half + at, block, 1)
        return mine, other

    own = to_all(teacher_hidden[0], Z).reshape(nz * piece, -1)
    turns = [0] + [k for k in range(1, ny) if k != ny // 2] + [ny // 2]
    hidden = [moved(own, Y, k) if k else own for k in turns]

    w = [jnp.concatenate(columns(student_weight, k), axis=1) for k in range(nx)]
    h = [student_hidden] * nx
    for k in range(1, nx):
        h[k] = moved(student_hidden, X, k)
        w[k] = moved(w[k], X, k)

    w_turned, h_turned = student_weight.T, student_hidden.T
    parts = [[] for _ in range(nx)]
    full = None
    for i, b in enumerate(hidden):
        if i == 1:
            b, w_turned, h_turned, _ = lax.optimization_barrier((b, w_turned, h_turned, full))
        elif i == ny - 1:
            b, parts, _ = lax.optimization_barrier((b, parts, full))
        elif i:
            b, _ = lax.optimization_barrier((b, full))
        full = dot(b, teacher_weight[0])
        theirs = moved(lax.dynamic_slice_in_dim(full, (1 - d) * half, half, 1), D, 1)
        for k in range(nx):
            at = lax.rem(x + k, nx) * block
            part = lax.dynamic_slice_in_dim(full, d * half + at, block, 1)
            part += lax.dynamic_slice_in_dim(theirs, at, block, 1)
            parts[k].append(part.astype(BF16))
    slots = []
    for k in range(nx):
        part = jnp.concatenate(parts[k], axis=0)
        slots.append(moved(part, X, k) if k else part)
    slots = jnp.concatenate(slots, axis=0)

    both = dot(h[0], w[0])
    for k in range(1, nx):
        both += dot(h[k], w[k])
    student = both[:, :block] + moved(both[:, block:], D, 1)

    sequence = jnp.arange(seqs, dtype=jnp.int32)
    same_before = (teacher_of_seq[None, :] == teacher_of_seq[:, None]) & (
        sequence[None, :] < sequence[:, None]
    )
    earlier = jnp.sum(same_before.astype(jnp.int32), axis=1)
    from_x = lax.rem(x - teacher_of_seq + nx, nx)
    turn = lax.rem(y - jnp.arange(ny, dtype=jnp.int32) + ny, ny)
    from_y = sum(jnp.where(turn == k, i, 0) for i, k in enumerate(turns))
    source = (from_x * (ny * nz) + earlier)[:, None] + (from_y * nz)[None, :]
    teacher = jnp.take(slots.reshape(-1, piece, block), source.reshape(-1), axis=0)
    teacher = teacher.reshape(rows, block).astype(F32)

    tm = jnp.max(teacher, axis=1)
    sm = jnp.max(student, axis=1)
    te = jnp.exp(teacher - tm[:, None])
    total = jnp.sum(te, axis=1)
    stats = jnp.stack(
        [
            tm + jnp.log(total),
            jnp.sum(te * (teacher - student), axis=1) / total,
            sm + jnp.log(jnp.sum(jnp.exp(student - sm[:, None]), axis=1)),
        ]
    )
    stats = merged(to_all(stats, (X, D)))
    kl_block = rows // (nx * nd)

    def own_rows(values):
        return lax.dynamic_slice_in_dim(values, (x * nd + d) * kl_block, kl_block, values.ndim - 1)

    all_stats = to_all(jnp.concatenate([stats[0], stats[2], own_rows(stats[1])]), (Z, Y))
    teacher_part = all_stats[:, :rows]
    teacher_lse, student_lse = lse(teacher_part), lse(all_stats[:, rows : 2 * rows])

    gradient = (
        vocab_total
        * (jnp.exp(student - student_lse[:, None]) - jnp.exp(teacher - teacher_lse[:, None]))
    ).astype(BF16)

    share = jnp.exp(own_rows(teacher_part) - own_rows(teacher_lse))
    cross = jnp.sum(all_stats[:, 2 * rows :] * share, axis=0)
    kl_rows = cross - own_rows(teacher_lse) + own_rows(student_lse)

    near = [gradient] + [moved(gradient, X, k) for k in range(1, nx)]
    everything = near + [moved(g, D, 1) for g in near]
    chip = lax.rem(x - jnp.arange(nx, dtype=jnp.int32) + nx, nx) * block
    at = jnp.concatenate([chip + d * half, chip + (1 - d) * half])
    partial = product(everything, [w_turned], BF16, at)

    piece_rows = rows // (nz * ny)
    by_y = partial.reshape(nz, ny, piece_rows, features)
    total = 0.0
    for k in range(ny):
        part = lax.dynamic_index_in_dim(by_y, lax.rem(y + k, ny), 1, keepdims=False)
        total += (moved(part, Y, k) if k else part).astype(F32)
    arrived = lax.all_to_all(total.astype(BF16), Z, 0, 0, tiled=True)
    grad_hidden = arrived.astype(F32).sum(axis=0).astype(BF16)

    grad_weight = weight_gradient(at, h_turned, everything)
    return (kl_rows, grad_weight, grad_hidden)


def solution(mesh):
    split = Mesh(
        mesh.devices.reshape(mesh.shape["teacher"], mesh.shape["dp"], 8, 4), (X, D, Z, Y)
    )
    return jax.shard_map(
        shards,
        mesh=split,
        in_specs=(
            P(),
            P(X, (Z, Y), D),
            P(X, D, (Z, Y)),
            P(None, (X, D)),
            P((X, D), (Z, Y)),
        ),
        out_specs=(P((X, D)), P((X, D), (Z, Y)), P((Z, Y), (X, D))),
        check_vma=False,
    )
```
